32 devices in a mesh: leaf: 2 (over x), row: 4 (over z), col: 4 (over y, core).
Axes of the slice: x: 2, y: 2, z: 4, core: 2. Of those that a mesh axis runs over, the one named last changes fastest.
Arguments:
- panels: float32 [4, 1024, 6144], P('leaf', 'col'), may hold values from -0.75 to 0.75
- tile_index: int32 [4, 48], P('leaf'), may hold values from 0 to 63, as said below
- front: float32 [8192, 4, 2, 1024], P('row', 'col', 'leaf'), may hold values from -4 to 4, as said below
- diag_inverses: float32 [4, 128, 128], replicated, may hold values from -0.03 to 0.18
Outputs:
- factored: float32 [8192, 4, 2, 1024], P('row', 'col', 'leaf')
The draws below stay inside these ranges and needn't reach their ends.
Inputs may be any that keep to these rules, and one draw needn't show every extreme that they name: `tile_index`: each row lists 48 distinct parent tiles in increasing order; 0 and 63 are always among them. Read as a 8192 x 8192 matrix, front is symmetric.
All inputs are finite; a program needn't handle non-finite values.
Results may differ from the reference program's by a relative error of at most 0.0003.
Values sent between devices are 32-bit elements; how exact they have to be, the bound alone decides.
A program may use at most 192 MiB of HBM per device.

```python
import jax
import jax.numpy as jnp
from jax import lax

TILE = 128
NT_C = 48
NT_P = 64
PT = 4
W = 1024
CHILDREN = 4
NU = 6144
NP = 8192
PW = 512
HB = 1024


def draw_tile_index(key, part):

    def one_child(sub):
        inner = jax.random.permutation(sub, NT_P - 2)[:NT_C - 2] + 1
        ends = jnp.array([0, NT_P - 1], dtype=jnp.int32)
        return jnp.sort(jnp.concatenate([ends, inner.astype(jnp.int32)]))
    child_keys = jax.random.split(key, CHILDREN)
    return jax.vmap(one_child)(child_keys).astype(jnp.int32)


def draw_front(key, part):
    base = jnp.clip(jax.random.normal(key, (NP, NP), jnp.float32), -4.0, 4.0)
    symmetric = 0.5 * (base + base.T)
    return symmetric.reshape(NP, NP // (2 * HB), 2, HB)


def draw_diag_inverses(key, part):
    spread = 0.075 / TILE ** 0.5
    noise = spread * jax.random.normal(key, (PT, TILE, TILE), jnp.float32)
    noise = jnp.clip(noise, -0.03, 0.03)
    return 0.15 * jnp.eye(TILE, dtype=jnp.float32)[None, :, :] + noise


def block_scale(own_key, shape, cuts, smallest, largest):
    loudness = 1.0
    for axis_at, parts in cuts:
        heights = jax.random.uniform(jax.random.fold_in(jax.random.fold_in(own_key, 6), axis_at), (parts,), jnp.float32, smallest / len(cuts), largest / len(cuts))
        loudness = loudness * jnp.repeat(jnp.exp(heights), shape[axis_at] // parts).reshape((-1,) + (1,) * (len(shape) - 1 - axis_at))
    return loudness


def centred(key, dims, width, bound, pieces=(), held_as=jnp.bfloat16):
    entries = width * jax.random.normal(key, dims, jnp.float32)
    if pieces:
        entries = entries * block_scale(key, dims, pieces, -0.22, 0.18)
    return jnp.clip(entries, -bound, bound).astype(held_as)


def setup_inputs(seed: int = 0) -> dict:
    seeds = jax.random.split(jax.random.key(seed), 5)
    panels = centred(seeds[0], (CHILDREN, W, NU), 0.125, 0.75, ((0, 2), (1, 4)), jnp.float32)
    tile_index = draw_tile_index(jax.random.fold_in(seeds[4], 71), 0)
    front = draw_front(jax.random.fold_in(seeds[4], 71), 0)
    diag_inverses = draw_diag_inverses(jax.random.fold_in(seeds[4], 71), 0)
    return {"panels": panels, "tile_index": tile_index, "front": front, "diag_inverses": diag_inverses}


HIGHEST = lax.Precision.HIGHEST


def blockwise(stacked, diag_inverses):
    tile_rows = diag_inverses.shape[1]
    solved = []
    for column_tile in range(diag_inverses.shape[0]):
        lower = column_tile * tile_rows
        current = stacked[:, lower:lower + tile_rows]
        if column_tile > 0:
            earlier = jnp.concatenate(solved, axis=1)
            current = current - jnp.dot(earlier, earlier[lower:lower + tile_rows].T, precision=HIGHEST, preferred_element_type=jnp.float32)
        solved.append(jnp.dot(current, diag_inverses[column_tile], precision=HIGHEST, preferred_element_type=jnp.float32))
    return jnp.concatenate(solved, axis=1)


def reference(panels, tile_index, front, diag_inverses):
    whole_front = front.reshape(NP, NP)
    offsets = jnp.arange(TILE, dtype=jnp.int32)

    def add_child(running, inputs):
        panel_rows, positions = inputs
        contribution = jnp.dot(panel_rows.T, panel_rows, precision=HIGHEST, preferred_element_type=jnp.float32)
        spots = (positions.astype(jnp.int32)[:, None] * TILE + offsets[None, :]).reshape(NU).astype(jnp.int32)
        return running.at[spots[:, None], spots[None, :]].add(-contribution), None

    assembled, unused = lax.scan(add_child, whole_front, (panels, tile_index))
    factor = blockwise(assembled[:, :PW], diag_inverses)
    remainder = assembled[:, PW:] - jnp.dot(factor, factor[PW:].T, precision=HIGHEST, preferred_element_type=jnp.float32)
    return jnp.concatenate([factor, remainder], axis=1).reshape(NP, NP // (2 * HB), 2, HB)
```

```python
import jax
import jax.numpy as jnp
from jax import lax
from jax.experimental import pallas as pl
from jax.experimental.pallas import tpu as pltpu
from jax.sharding import PartitionSpec as P

EXACT = lax.Precision.HIGH
HIGHEST = lax.Precision.HIGHEST


def spread(block, axis, holder):
    block = jnp.where(lax.axis_index(axis) == holder, block, jnp.zeros_like(block))
    return lax.psum(block, axis)


def blockwise(stacked, diag_inverses):
    tile_rows = diag_inverses.shape[1]
    solved = []
    for column_tile in range(diag_inverses.shape[0]):
        lower = column_tile * tile_rows
        current = stacked[:, lower : lower + tile_rows]
        if column_tile > 0:
            earlier = jnp.concatenate(solved, axis=1)
            current = current - jnp.dot(
                earlier,
                earlier[lower : lower + tile_rows].T,
                precision=HIGHEST,
                preferred_element_type=jnp.float32,
            )
        solved.append(
            jnp.dot(
                current,
                diag_inverses[column_tile],
                precision=HIGHEST,
                preferred_element_type=jnp.float32,
            )
        )
    return jnp.concatenate(solved, axis=1)


def select_kernel(source_ref, present_ref, panels_ref, placed_ref):
    child = pl.program_id(0)
    tiles_out = source_ref.shape[1]
    tile_rows = placed_ref.shape[2] // tiles_out
    for tile in range(tiles_out):
        start = pl.multiple_of(source_ref[child, tile] * tile_rows, tile_rows)
        lanes = pl.ds(tile * tile_rows, tile_rows)

        @pl.when(present_ref[child, tile] > 0)
        def _():
            placed_ref[0, :, lanes] = panels_ref[0, :, pl.ds(start, tile_rows)]

        @pl.when(present_ref[child, tile] == 0)
        def _():
            placed_ref[0, :, lanes] = jnp.zeros((placed_ref.shape[1], tile_rows), jnp.float32)


def select_tiles(panels, tile_index, tiles_out, tile_rows):
    children, width, order = panels.shape
    wanted = lax.iota(jnp.int32, tiles_out)
    matches = tile_index[:, :, None] == wanted[None, None, :]
    places = lax.iota(jnp.int32, tile_index.shape[1])
    source = jnp.sum(jnp.where(matches, places[None, :, None], 0), axis=1).astype(jnp.int32)
    present = jnp.any(matches, axis=1).astype(jnp.int32)
    strip = min(width, 64)
    return pl.pallas_call(
        select_kernel,
        grid_spec=pltpu.PrefetchScalarGridSpec(
            num_scalar_prefetch=2,
            grid=(children, width // strip),
            in_specs=[pl.BlockSpec((1, strip, order), lambda k, w, *_: (k, w, 0))],
            out_specs=pl.BlockSpec((1, strip, tiles_out * tile_rows), lambda k, w, *_: (k, w, 0)),
        ),
        out_shape=jax.ShapeDtypeStruct((children, width, tiles_out * tile_rows), jnp.float32),
    )(source, present, panels)


def exchange(axis, mask):
    return [(here, here ^ mask) for here in range(lax.axis_size(axis))]


def swap_rows(own_rows):
    held = {0: own_rows}
    mask = lax.axis_size("col") // 2
    while mask > 0:
        for key in list(held):
            held[key ^ mask] = lax.ppermute(held[key], "col", exchange("col", mask))
        mask //= 2
    return [held[key] for key in sorted(held)]


def far_pieces(flat, half, half_width):
    col_index = lax.axis_index("col")
    share = flat.shape[0] // lax.axis_size("row")
    pieces = []
    for mask in range(lax.axis_size("col")):
        start = (lax.bitwise_xor(col_index, mask) * 2 + half) * half_width
        if mask < 2:
            piece = lax.dynamic_slice_in_dim(flat, start, half_width, 1)
        else:
            corner = (lax.axis_index("row") * share, start)
            piece = lax.dynamic_slice(flat, corner, (share, half_width))
        if mask > 0:
            piece = lax.ppermute(piece, "col", exchange("col", mask))
        pieces.append(piece)
    return pieces


def join_pieces(pieces):
    joined = pieces[:2] + [lax.all_gather(piece, "row", axis=0, tiled=True) for piece in pieces[2:]]
    return jnp.concatenate(joined, axis=0)


def contract(left, right):
    return lax.dot_general(
        left,
        right,
        (((0,), (0,)), ((), ())),
        precision=EXACT,
        preferred_element_type=jnp.float32,
    )


def local(panels, tile_index, front, diag_inverses):
    row_index = lax.axis_index("row")
    col_index = lax.axis_index("col")
    leaf_index = lax.axis_index("leaf")
    tile_rows = diag_inverses.shape[1]
    panel_width = diag_inverses.shape[0] * tile_rows
    local_front = front.reshape(front.shape[0], front.shape[3])
    block_rows = local_front.shape[0]
    half_width = local_front.shape[1]
    tiles_block = block_rows // tile_rows
    all_rows = select_tiles(panels, tile_index, lax.axis_size("row") * tiles_block, tile_rows)
    flat = all_rows.reshape(all_rows.shape[0] * all_rows.shape[1], all_rows.shape[2])
    own_rows = lax.dynamic_slice_in_dim(flat, row_index * block_rows, block_rows, 1)
    near = far_pieces(flat, 1 - leaf_index, half_width)
    flat, near = lax.optimization_barrier((flat, near))
    gathered = jnp.concatenate(swap_rows(own_rows), axis=0)
    other_columns = join_pieces(near)
    own_columns = join_pieces(far_pieces(flat, leaf_index, half_width))
    chunk = block_rows // 2
    arrived = []
    for start in range(0, block_rows, chunk):
        sent = contract(gathered[:, start : start + chunk], other_columns)
        arrived.append(lax.ppermute(sent, "leaf", exchange("leaf", 1)))
    summed = contract(gathered, own_columns) + jnp.concatenate(arrived, axis=0)
    assembled = local_front - summed
    upper_rows = spread(assembled[:panel_width], "row", 0)
    if half_width >= panel_width:
        holds = (col_index == 0) & (leaf_index == 0)
        own_part = assembled[:, :panel_width]
        own_part = jnp.where(holds, own_part, jnp.zeros_like(own_part))
        panel_slab = lax.psum(own_part, ("col", "leaf"))
        own_corner = own_part[:panel_width]
        own_corner = jnp.where(row_index == 0, own_corner, jnp.zeros_like(own_corner))
        corner = lax.psum(own_corner, ("row", "col", "leaf"))
    else:
        panel_top = spread(assembled, "col", 0)
        panel_slab = lax.all_gather(panel_top, "leaf", axis=1, tiled=True)[:, :panel_width]
        corner = spread(panel_slab[:panel_width], "row", 0)
    solved = blockwise(jnp.concatenate([corner, panel_slab, upper_rows.T], axis=0), diag_inverses)
    factor = solved[panel_width : panel_width + block_rows]
    far_factor = solved[panel_width + block_rows :]
    trailing = assembled - jnp.dot(
        factor, far_factor.T, precision=EXACT, preferred_element_type=jnp.float32
    )
    padded = jnp.pad(factor, ((0, 0), (0, 2 * half_width - panel_width)))
    own_panel = lax.dynamic_slice_in_dim(padded, leaf_index * half_width, half_width, 1)
    columns = (col_index * 2 + leaf_index) * half_width + lax.iota(jnp.int32, half_width)
    result = jnp.where(columns[None, :] < panel_width, own_panel, trailing)
    return result.reshape(block_rows, 1, 1, half_width)


def solution(mesh):
    placed = (P("leaf", "col", None), P("leaf", None), P("row", "col", "leaf", None), P())
    return jax.shard_map(
        local, mesh=mesh, in_specs=placed, out_specs=P("row", "col", "leaf", None), check_vma=False
    )
```

```python
import jax
import jax.numpy as jnp
from jax import lax
from jax.experimental import pallas as pl
from jax.experimental.pallas import tpu as pltpu
from jax.sharding import PartitionSpec as P

EXACT = lax.Precision.HIGH
HIGHEST = lax.Precision.HIGHEST


def spread(block, axis, holder):
    block = jnp.where(lax.axis_index(axis) == holder, block, jnp.zeros_like(block))
    return lax.psum(block, axis)


def blockwise(stacked, diag_inverses):
    tile_rows = diag_inverses.shape[1]
    solved = []
    for column_tile in range(diag_inverses.shape[0]):
        lower = column_tile * tile_rows
        current = stacked[:, lower : lower + tile_rows]
        if column_tile > 0:
            earlier = jnp.concatenate(solved, axis=1)
            current = current - jnp.dot(
                earlier,
                earlier[lower : lower + tile_rows].T,
                precision=HIGHEST,
                preferred_element_type=jnp.float32,
            )
        solved.append(
            jnp.dot(
                current,
                diag_inverses[column_tile],
                precision=HIGHEST,
                preferred_element_type=jnp.float32,
            )
        )
    return jnp.concatenate(solved, axis=1)


def select_kernel(source_ref, present_ref, panels_ref, placed_ref):
    child = pl.program_id(0)
    tiles_out = source_ref.shape[1]
    tile_rows = placed_ref.shape[2] // tiles_out
    for tile in range(tiles_out):
        start = pl.multiple_of(source_ref[child, tile] * tile_rows, tile_rows)
        lanes = pl.ds(tile * tile_rows, tile_rows)

        @pl.when(present_ref[child, tile] > 0)
        def _():
            placed_ref[0, :, lanes] = panels_ref[0, :, pl.ds(start, tile_rows)]

        @pl.when(present_ref[child, tile] == 0)
        def _():
            placed_ref[0, :, lanes] = jnp.zeros((placed_ref.shape[1], tile_rows), jnp.float32)


def select_tiles(panels, tile_index, tiles_out, tile_rows):
    children, width, order = panels.shape
    wanted = lax.iota(jnp.int32, tiles_out)
    matches = tile_index[:, :, None] == wanted[None, None, :]
    places = lax.iota(jnp.int32, tile_index.shape[1])
    source = jnp.sum(jnp.where(matches, places[None, :, None], 0), axis=1).astype(jnp.int32)
    present = jnp.any(matches, axis=1).astype(jnp.int32)
    strip = min(width, 64)
    return pl.pallas_call(
        select_kernel,
        grid_spec=pltpu.PrefetchScalarGridSpec(
            num_scalar_prefetch=2,
            grid=(children, width // strip),
            in_specs=[pl.BlockSpec((1, strip, order), lambda k, w, *_: (k, w, 0))],
            out_specs=pl.BlockSpec((1, strip, tiles_out * tile_rows), lambda k, w, *_: (k, w, 0)),
        ),
        out_shape=jax.ShapeDtypeStruct((children, width, tiles_out * tile_rows), jnp.float32),
    )(source, present, panels)


def exchange(axis, mask):
    return [(here, here ^ mask) for here in range(lax.axis_size(axis))]


def swap_rows(own_rows):
    held = {0: own_rows}
    mask = lax.axis_size("col") // 2
    while mask > 0:
        for key in list(held):
            held[key ^ mask] = lax.ppermute(held[key], "col", exchange("col", mask))
        mask //= 2
    return [held[key] for key in sorted(held)]


def far_pieces(flat, half, half_width):
    col_index = lax.axis_index("col")
    share = flat.shape[0] // lax.axis_size("row")
    pieces = []
    for mask in range(lax.axis_size("col")):
        start = (lax.bitwise_xor(col_index, mask) * 2 + half) * half_width
        if mask < 2:
            piece = lax.dynamic_slice_in_dim(flat, start, half_width, 1)
        else:
            corner = (lax.axis_index("row") * share, start)
            piece = lax.dynamic_slice(flat, corner, (share, half_width))
        if mask > 0:
            piece = lax.ppermute(piece, "col", exchange("col", mask))
        pieces.append(piece)
    return pieces


def join_pieces(pieces):
    joined = pieces[:2] + [lax.all_gather(piece, "row", axis=0, tiled=True) for piece in pieces[2:]]
    return jnp.concatenate(joined, axis=0)


def contract(left, right):
    return lax.dot_general(
        left,
        right,
        (((0,), (0,)), ((), ())),
        precision=EXACT,
        preferred_element_type=jnp.float32,
    )


def local(panels, tile_index, front, diag_inverses):
    row_index = lax.axis_index("row")
    col_index = lax.axis_index("col")
    leaf_index = lax.axis_index("leaf")
    tile_rows = diag_inverses.shape[1]
    panel_width = diag_inverses.shape[0] * tile_rows
    local_front = front.reshape(front.shape[0], front.shape[3])
    block_rows = local_front.shape[0]
    half_width = local_front.shape[1]
    tiles_block = block_rows // tile_rows
    all_rows = select_tiles(panels, tile_index, lax.axis_size("row") * tiles_block, tile_rows)
    flat = all_rows.reshape(all_rows.shape[0] * all_rows.shape[1], all_rows.shape[2])
    own_rows = lax.dynamic_slice_in_dim(flat, row_index * block_rows, block_rows, 1)
    near = far_pieces(flat, 1 - leaf_index, half_width)
    flat, near = lax.optimization_barrier((flat, near))
    gathered = jnp.concatenate(swap_rows(own_rows), axis=0)
    other_columns = join_pieces(near)
    own_columns = join_pieces(far_pieces(flat, leaf_index, half_width))
    chunk = block_rows // 2
    arrived = []
    for start in range(0, block_rows, chunk):
        sent = contract(gathered[:, start : start + chunk], other_columns)
        arrived.append(lax.ppermute(sent, "leaf", exchange("leaf", 1)))
    summed = contract(gathered, own_columns) + jnp.concatenate(arrived, axis=0)
    assembled = local_front - summed
    upper_rows = spread(assembled[:panel_width], "row", 0)
    if half_width >= panel_width:
        holds = (col_index == 0) & (leaf_index == 0)
        own_part = assembled[:, :panel_width]
        own_part = jnp.where(holds, own_part, jnp.zeros_like(own_part))
        panel_slab = lax.psum(own_part, ("col", "leaf"))
    else:
        panel_top = spread(assembled, "col", 0)
        panel_slab = lax.all_gather(panel_top, "leaf", axis=1, tiled=True)[:, :panel_width]
    corner = spread(panel_slab[:panel_width], "row", 0)
    solved = blockwise(jnp.concatenate([corner, panel_slab, upper_rows.T], axis=0), diag_inverses)
    factor = solved[panel_width : panel_width + block_rows]
    far_factor = solved[panel_width + block_rows :]
    trailing = assembled - jnp.dot(
        factor, far_factor.T, precision=EXACT, preferred_element_type=jnp.float32
    )
    padded = jnp.pad(factor, ((0, 0), (0, 2 * half_width - panel_width)))
    own_panel = lax.dynamic_slice_in_dim(padded, leaf_index * half_width, half_width, 1)
    columns = (col_index * 2 + leaf_index) * half_width + lax.iota(jnp.int32, half_width)
    result = jnp.where(columns[None, :] < panel_width, own_panel, trailing)
    return result.reshape(block_rows, 1, 1, half_width)


def solution(mesh):
    placed = (P("leaf", "col", None), P("leaf", None), P("row", "col", "leaf", None), P())
    return jax.shard_map(
        local, mesh=mesh, in_specs=placed, out_specs=P("row", "col", "leaf", None), check_vma=False
    )
```
